32 devices in a mesh: area: 4 (over y, core), depth: 8 (over z, x).
Axes of the slice: x: 2, y: 2, z: 4, core: 2. Of those that a mesh axis runs over, the one named last changes fastest.
Arguments:
- field: float32 [256, 256, 512], P('depth', 'area'), may hold values from -6 to 6
- materials: int32 [256, 256, 512], P('depth', 'area'), may hold values from 0 to 15
- tf_table: float32 [4, 16], replicated, may hold values from 0 to 1, as said below
- view_order: int32 [2, 8], replicated, may hold values from 0 to 7, each once within a row
- shear_offset: int32 [8], replicated, may hold values from 0 to 63, as said below
Outputs:
- image: float32 [2, 4, 256, 512], P(None, None, ('area', 'depth'))
The draws below stay inside these ranges and needn't reach their ends.
Inputs may be any that keep to these rules, and one draw needn't show every extreme that they name: `shear_offset`: every entry lies in 0 to 63; some layer has offset 0 and some layer has offset 64 - 1. `view_order`: each row is a permutation of the depth layers. `tf_table`: the colour rows lie in 0.05 to 0.6; the opacity row lies in 0.02 / 32 to 0.5 / 32.
All inputs are finite; a program needn't handle non-finite values.
Results may differ from the reference program's by a relative error of at most 0.0003.
Values sent between devices are 32-bit elements; how exact they have to be, the bound alone decides.
No kernel may reach another device: no remote copies, remote signals or barrier semaphores. Data moves between devices by JAX's collectives and lax.ppermute only.
A program may use at most 128 MiB of HBM per device.

```python
import jax
import jax.numpy as jnp
from jax import lax

BZ = 32
BY = 64
BX = 512
TFN = 16
NZ = 256
NY = 256
N_DEPTH = 8


def draw_shear_offset(key, part):
    first_key = jax.random.fold_in(key, 11)
    second_key = jax.random.fold_in(key, 12)
    values = jax.random.randint(first_key, (N_DEPTH,), 0, BY, dtype=jnp.int32)
    places = jax.random.permutation(second_key, N_DEPTH)
    values = values.at[places[0]].set(BY - 1)
    values = values.at[places[1]].set(0)
    return values.astype(jnp.int32)


def draw_tf_table(key, part):
    colour_key = jax.random.fold_in(key, 21)
    opacity_key = jax.random.fold_in(key, 22)
    colours = jax.random.uniform(colour_key, (3, TFN), jnp.float32, 0.05, 0.6)
    opacities = jax.random.uniform(opacity_key, (1, TFN), jnp.float32, 0.02, 0.5) / jnp.float32(BZ)
    return jnp.concatenate([colours, opacities], axis=0).astype(jnp.float32)


def set_ends(values, rng, smallest, top_value):
    longest = values.shape.index(max(values.shape))
    spots = []
    for shift in (0, 1):
        where = [jax.random.randint(jax.random.fold_in(rng, axis), (), 0, length) for axis, length in enumerate(values.shape)]
        where[longest] = (where[longest] + shift) % values.shape[longest]
        spots.append(tuple(where))
    return values.at[spots[0]].set(smallest).at[spots[1]].set(top_value)


def steps_of(rng, dims, split, smallest, top_value):
    gain = 1.0
    for axis_at, shards_of in split:
        draws = jax.random.uniform(jax.random.fold_in(jax.random.fold_in(rng, 6), axis_at), (shards_of,), jnp.float32, smallest / len(split), top_value / len(split))
        gain = gain * jnp.repeat(jnp.exp(draws), dims[axis_at] // shards_of).reshape((-1,) + (1,) * (len(dims) - 1 - axis_at))
    return gain


def scatter_about(stream_key, shape, scale, most, cuts=(), kind=jnp.bfloat16):
    entries = scale * jax.random.normal(stream_key, shape, jnp.float32)
    if cuts:
        entries = entries * steps_of(stream_key, shape, cuts, -0.22, 0.18)
    return jnp.clip(entries, -most, most).astype(kind)


def setup_inputs(seed: int = 0) -> dict:
    arg_keys = jax.random.split(jax.random.key(seed), 6)
    return {
        "field": scatter_about(arg_keys[0], (NZ, NY, BX), 1.0, 6.0, ((0, 8), (1, 4)), jnp.float32),
        "materials": set_ends(jax.random.randint(arg_keys[1], (NZ, NY, BX), 0, TFN), jax.random.fold_in(arg_keys[1], 1), 0, TFN - 1).astype(jnp.int32),
        "tf_table": draw_tf_table(jax.random.fold_in(arg_keys[5], 71), 0),
        "view_order": jax.vmap(lambda own: jax.random.permutation(own, N_DEPTH))(jax.random.split(arg_keys[3], 2)).reshape((2, N_DEPTH)).astype(jnp.int32),
        "shear_offset": draw_shear_offset(jax.random.fold_in(arg_keys[5], 71), 0),
    }


def classify(padded, materials, tf_table):
    widened = jnp.pad(padded, ((0, 0), (0, 0), (1, 1)))
    center = widened[1:-1, 1:-1, 1:-1]
    grad_z = 0.5 * (widened[2:, 1:-1, 1:-1] - widened[:-2, 1:-1, 1:-1])
    grad_y = 0.5 * (widened[1:-1, 2:, 1:-1] - widened[1:-1, :-2, 1:-1])
    grad_x = 0.5 * (widened[1:-1, 1:-1, 2:] - widened[1:-1, 1:-1, :-2])
    grad_sq = grad_z * grad_z + grad_y * grad_y + grad_x * grad_x
    shade = 0.3 + 0.7 * jnp.abs(0.48 * grad_z + 0.6 * grad_y + 0.64 * grad_x) / jnp.sqrt(grad_sq + 1.0)
    looked = []
    for channel in range(4):
        total = jnp.zeros(materials.shape, jnp.float32)
        for entry in range(tf_table.shape[1]):
            total = total + jnp.where(materials == entry, tf_table[channel, entry], jnp.float32(0.0))
        looked.append(total)
    opacity_cell = looked[3] * (1.0 - jnp.exp(-0.25 * (center * center + grad_sq)))
    colour_cell = jnp.stack(looked[:3]) * (shade * opacity_cell)[None]
    return (colour_cell, opacity_cell)

def march(colour_cell, opacity_cell):
    log_keep = jnp.log1p(-opacity_cell)
    before = jnp.exp(jnp.cumsum(log_keep, axis=0) - log_keep)
    colour = lax.optimization_barrier(jnp.sum(colour_cell * before[None], axis=1))
    opacity = 1.0 - jnp.exp(lax.optimization_barrier(jnp.sum(log_keep, axis=0)))
    return jnp.concatenate([colour, opacity[None]], axis=0)

def composite(stack, view_order):
    results = []
    for view_idx in range(2):
        sequence = jnp.take(stack[:, view_idx], view_order[view_idx], axis=0)

        def over_step(state_pair, layer_img):
            colour, opacity = state_pair
            colour = colour + (1.0 - opacity)[None] * layer_img[:3]
            opacity = opacity + (1.0 - opacity) * layer_img[3]
            return ((colour, opacity), None)
        start = (jnp.zeros((3,) + sequence.shape[2:], jnp.float32), jnp.zeros(sequence.shape[2:], jnp.float32))
        (colour, opacity), unused = lax.scan(over_step, start, sequence)
        results.append(jnp.concatenate([colour, opacity[None]], axis=0))
    return jnp.stack(results)

def reference(field, materials, tf_table, view_order, shear_offset):
    padded_all = jnp.pad(field, ((1, 1), (1, 1), (0, 0)))
    rows_all = field.shape[1]

    def one_layer(layer_idx):
        layer_idx = layer_idx.astype(jnp.int32)
        start = (layer_idx * BZ).astype(jnp.int32)
        zero = jnp.int32(0)
        block = lax.dynamic_slice(padded_all, (start, zero, zero), (BZ + 2, rows_all + 2, BX))
        mats = lax.dynamic_slice(materials, (start, zero, zero), (BZ, rows_all, BX))
        colour_cell, opacity_cell = classify(block, mats, tf_table)
        first = march(colour_cell, opacity_cell)
        second = march(colour_cell[:, ::-1], opacity_cell[::-1])
        spread = jnp.zeros((4, rows_all + BY, BX), jnp.float32)
        spread = lax.dynamic_update_slice(spread, second, (zero, shear_offset[layer_idx].astype(jnp.int32), zero))
        return jnp.stack([first, spread[:, :rows_all]])
    stack = lax.map(one_layer, jnp.arange(N_DEPTH, dtype=jnp.int32))
    return composite(stack, view_order)
```

```python
import functools

import jax
import jax.numpy as jnp
from jax import lax
from jax.experimental import pallas as pl
from jax.experimental.pallas import tpu as pltpu
from jax.sharding import PartitionSpec as P

LANES, SUB = 128, 8
LOG2E = 1.4426950408889634
SHADE_UNIT = 0.7 * 0.5 * 0.48

LOOKUP = lax.GatherDimensionNumbers(
    offset_dims=(),
    collapsed_slice_dims=(1,),
    start_index_map=(1,),
    operand_batching_dims=(0,),
    start_indices_batching_dims=(0,),
)


def lookup(table, idx):
    return lax.gather(
        table, idx[:, :, None], LOOKUP, (1, 1), mode=lax.GatherScatterMode.PROMISE_IN_BOUNDS
    )


def put(ref, tile, channel, cols, value):
    own = ref.shape[2]
    if own >= SUB:
        per = own // SUB
        if per == 1:
            ref[tile, channel, :, cols] = value
        else:
            ref[tile // per, channel, pl.ds(pl.multiple_of((tile % per) * SUB, SUB), SUB), cols] = value
    else:
        for part in range(SUB // own):
            ref[tile * (SUB // own) + part, channel, :, cols] = value[part * own : (part + 1) * own]


def march_body(
    offset, field_hbm, mats_hbm, z_lo, z_hi, y_lo, y_hi, table,
    first, own, spill, field, mats, weight, keep, spread, sems,
):
    depth, rows, width = field_hbm.shape
    strips = width // LANES
    cols = [slice(j * LANES, (j + 1) * LANES) for j in range(strips)]
    copies = []
    for j in range(strips):
        lanes = pl.ds(j * LANES, LANES)
        copies.append(
            pltpu.make_async_copy(
                field_hbm.at[:, :, lanes],
                field.at[pl.ds(1, depth), j, pl.ds(SUB, rows), :],
                sems.at[0, j],
            )
        )
        copies.append(pltpu.make_async_copy(mats_hbm.at[:, :, lanes], mats.at[:, j], sems.at[1, j]))
    for copy in copies:
        copy.start()
    for j in range(strips):
        field[0, j, SUB : SUB + rows, :] = z_lo[:, cols[j]]
        field[depth + 1, j, SUB : SUB + rows, :] = z_hi[:, cols[j]]
    spread[...] = jnp.zeros_like(spread)
    for copy in copies:
        copy.wait()
    for j in range(strips):
        field[1 : depth + 1, j, SUB - 1, :] = y_lo[:, cols[j]]
        field[1 : depth + 1, j, SUB + rows, :] = y_hi[:, cols[j]]
    lane = lax.broadcasted_iota(jnp.int32, (SUB, LANES), 1)
    left_end = lane == 0
    right_end = lane == LANES - 1
    zero = jnp.zeros((SUB, LANES), jnp.float32)
    shift = offset[0]

    def tile(i, unused):
        r = pl.multiple_of(i * SUB, SUB)
        opacity_row = jnp.broadcast_to(table[3:4, :], (SUB, LANES))

        def cells(z, unused):
            f = [field[z + 1, j, pl.ds(SUB + r, SUB), :] for j in range(strips)]
            from_left = [pltpu.roll(v, 1, 1) for v in f]
            from_right = [pltpu.roll(v, LANES - 1, 1) for v in f]
            for j in range(strips):
                above = field[z + 2, j, pl.ds(SUB + r, SUB), :]
                below = field[z, j, pl.ds(SUB + r, SUB), :]
                dz = above - below
                dy = (
                    field[z + 1, j, pl.ds(SUB + r + 1, SUB), :]
                    - field[z + 1, j, pl.ds(SUB + r - 1, SUB), :]
                )
                left = jnp.where(left_end, from_left[j - 1] if j else zero, from_left[j])
                right = jnp.where(
                    right_end, from_right[j + 1] if j < strips - 1 else zero, from_right[j]
                )
                dx = right - left
                grad_sq = 0.25 * (dz * dz + dy * dy + dx * dx)
                slope = jnp.abs(dz + (0.6 / 0.48) * dy + (0.64 / 0.48) * dx)
                shade = (0.3 / SHADE_UNIT) + slope * lax.rsqrt(grad_sq + 1.0)
                clear = jnp.exp2((-0.25 * LOG2E) * (f[j] * f[j] + grad_sq))
                most = lookup(opacity_row, mats[z, j, pl.ds(r, SUB), :])
                opacity = most - most * clear
                weight[z, j] = shade * opacity
                keep[z, j] = 1.0 - opacity
            return unused

        lax.fori_loop(0, depth, cells, 0, unroll=8)
        for j0 in range(0, strips, 2):
            colours = [jnp.broadcast_to(table[c : c + 1, :], (SUB, LANES)) for c in range(3)]

            def step(z, carry):
                result = []
                for k, (passed, front, back) in enumerate(carry):
                    j = j0 + k
                    w = weight[z, j]
                    kept = keep[z, j]
                    seen = w * passed
                    idx = mats[z, j, pl.ds(r, SUB), :]
                    looked = [lookup(t, idx) for t in colours]
                    result.append(
                        (
                            passed * kept,
                            [front[c] + looked[c] * seen for c in range(3)],
                            [back[c] * kept + looked[c] * w for c in range(3)],
                        )
                    )
                return result

            start = [(zero + 1.0, [zero] * 3, [zero] * 3)] * 2
            done = lax.fori_loop(0, depth, step, start, unroll=8)
            for k, (passed, front, back) in enumerate(done):
                j = j0 + k
                place = pl.ds(shift + r, SUB)
                for c in range(3):
                    put(first, i, c, cols[j], front[c])
                    spread[c, j, place, :] = back[c]
                put(first, i, 3, cols[j], 1.0 - passed)
                spread[3, j, place, :] = 1.0 - passed
        return unused

    lax.fori_loop(0, rows // SUB, tile, 0)

    def hand_out(i, unused):
        r = pl.multiple_of(i * SUB, SUB)
        for c in range(4):
            for j in range(strips):
                put(own, i, c, cols[j], spread[c, j, pl.ds(r, SUB), :])
                put(spill, i, c, cols[j], spread[c, j, pl.ds(rows + r, SUB), :])
        return unused

    lax.fori_loop(0, rows // SUB, hand_out, 0)


def march(offset, field, mats, z_lo, z_hi, y_lo, y_hi, table, receivers):
    depth, rows, width = field.shape
    strips = width // LANES
    vmem = pl.BlockSpec(memory_space=pltpu.VMEM)
    hbm = pl.BlockSpec(memory_space=pltpu.HBM)
    image = jax.ShapeDtypeStruct((receivers, 4, rows // receivers, width), jnp.float32)
    return pl.pallas_call(
        march_body,
        out_shape=(image, image, image),
        in_specs=[pl.BlockSpec(memory_space=pltpu.SMEM), hbm, hbm] + [vmem] * 5,
        out_specs=(vmem, vmem, vmem),
        scratch_shapes=[
            pltpu.VMEM((depth + 2, strips, rows + 2 * SUB, LANES), jnp.float32),
            pltpu.VMEM((depth, strips, rows, LANES), jnp.int32),
            pltpu.VMEM((depth, strips, SUB, LANES), jnp.float32),
            pltpu.VMEM((depth, strips, SUB, LANES), jnp.float32),
            pltpu.VMEM((4, strips, 2 * rows, LANES), jnp.float32),
            pltpu.SemaphoreType.DMA((2, strips)),
        ],
        compiler_params=pltpu.CompilerParams(vmem_limit_bytes=40 << 20),
        cost_estimate=pl.CostEstimate(flops=10**8, bytes_accessed=10**7, transcendentals=10**6),
        name="march",
    )(offset, field, mats, z_lo, z_hi, y_lo, y_hi, table)


def composite_body(order, *refs):
    out = refs[-1]
    for view, stack in enumerate(refs[:-1]):
        layers = stack.shape[0]
        seen = jnp.ones(stack.shape[2:], jnp.float32)
        colour = [jnp.zeros(stack.shape[2:], jnp.float32)] * 3
        for k in range(layers):
            layer = order[view, k]
            colour = [colour[c] + seen * stack[layer, c] for c in range(3)]
            seen = seen - seen * stack[layer, 3]
        for c in range(3):
            out[view, c] = colour[c]
        out[view, 3] = 1.0 - seen


def composite(order, stacks):
    vmem = pl.BlockSpec(memory_space=pltpu.VMEM)
    return pl.pallas_call(
        composite_body,
        out_shape=jax.ShapeDtypeStruct((len(stacks),) + stacks[0].shape[1:], jnp.float32),
        in_specs=[pl.BlockSpec(memory_space=pltpu.SMEM)] + [vmem] * len(stacks),
        out_specs=vmem,
        name="composite",
    )(order, *stacks)


def neighbours(block, axis, dim):
    count = lax.axis_size(axis)
    up = [(i, i + 1) for i in range(count - 1)]
    down = [(b, a) for a, b in up]
    size = block.shape[dim]
    low = lax.ppermute(lax.index_in_dim(block, size - 1, dim, keepdims=False), axis, up)
    high = lax.ppermute(lax.index_in_dim(block, 0, dim, keepdims=False), axis, down)
    return low, high


def shards(field, materials, tf_table, view_order, shear_offset):
    receivers = lax.axis_size("depth")
    y_lo, y_hi = neighbours(field, "area", 1)
    z_lo, z_hi = neighbours(field, "depth", 0)
    scaled = tf_table * jnp.array([[SHADE_UNIT]] * 3 + [[1.0]], jnp.float32)
    table = jnp.pad(scaled, ((0, 0), (0, LANES - tf_table.shape[1])))
    offset = lax.dynamic_slice_in_dim(shear_offset, lax.axis_index("depth"), 1)
    first, own, spill = march(offset, field, materials, z_lo, z_hi, y_lo, y_hi, table, receivers)
    columns = lax.axis_size("area")
    stack0 = lax.all_to_all(first, "depth", split_axis=0, concat_axis=0, tiled=True)
    arrived = lax.ppermute(spill, "area", [(i, i + 1) for i in range(columns - 1)])
    sheared = own + arrived
    stack1 = lax.all_to_all(sheared, "depth", split_axis=0, concat_axis=0, tiled=True)
    return composite(view_order, (stack0, stack1))


def solution(mesh):
    in_specs = (P("depth", "area", None), P("depth", "area", None), P(), P(), P())
    out_specs = P(None, None, ("area", "depth"), None)
    return jax.shard_map(shards, mesh=mesh, in_specs=in_specs, out_specs=out_specs, check_vma=False)
```

```python
import functools

import jax
import jax.numpy as jnp
from jax import lax
from jax.experimental import pallas as pl
from jax.experimental.pallas import tpu as pltpu
from jax.sharding import PartitionSpec as P

LANES, SUB, GROUP = 128, 8, 16
LOG2E = 1.4426950408889634
SHADE_UNIT = 0.7 * 0.5 * 0.48

LOOKUP = lax.GatherDimensionNumbers(
    offset_dims=(),
    collapsed_slice_dims=(0,),
    start_index_map=(0,),
    operand_batching_dims=(1,),
    start_indices_batching_dims=(1,),
)


def lookup(halves, idx):
    place = (idx & (SUB - 1))[:, :, None]
    low, high = (
        lax.gather(half, place, LOOKUP, (1, 1), mode=lax.GatherScatterMode.PROMISE_IN_BOUNDS)
        for half in halves
    )
    return jnp.where(idx >= SUB, high, low)


def put(ref, tile, channel, cols, value):
    own = ref.shape[2]
    if own >= SUB:
        per = own // SUB
        if per == 1:
            ref[tile, channel, :, cols] = value
        else:
            ref[tile // per, channel, pl.ds(pl.multiple_of((tile % per) * SUB, SUB), SUB), cols] = value
    else:
        for part in range(SUB // own):
            ref[tile * (SUB // own) + part, channel, :, cols] = value[part * own : (part + 1) * own]


def is_even(axis):
    return lax.rem(lax.axis_index(axis), 2) == 0


def edges_body(field_hbm, z_first, z_second, y_first, y_second, rim, sems):
    depth, rows, _ = field_hbm.shape
    z_even, y_even = is_even("depth"), is_even("area")
    copies = [
        pltpu.make_async_copy(field_hbm.at[jnp.where(z_even, depth - 1, 0)], z_first, sems.at[0]),
        pltpu.make_async_copy(field_hbm.at[jnp.where(z_even, 0, depth - 1)], z_second, sems.at[1]),
        pltpu.make_async_copy(field_hbm.at[:, pl.ds(0, SUB), :], rim.at[0], sems.at[2]),
        pltpu.make_async_copy(field_hbm.at[:, pl.ds(rows - SUB, SUB), :], rim.at[1], sems.at[3]),
    ]
    for copy in copies:
        copy.start()
    for copy in copies[2:]:
        copy.wait()
    low, high = rim[0, :, 0, :], rim[1, :, SUB - 1, :]
    y_first[...] = jnp.where(y_even, high, low)
    y_second[...] = jnp.where(y_even, low, high)
    for copy in copies[:2]:
        copy.wait()


def edges(field):
    depth, rows, width = field.shape
    vmem = pl.BlockSpec(memory_space=pltpu.VMEM)
    plane = jax.ShapeDtypeStruct((rows, width), jnp.float32)
    wall = jax.ShapeDtypeStruct((depth, width), jnp.float32)
    return pl.pallas_call(
        edges_body,
        out_shape=(plane, plane, wall, wall),
        in_specs=[pl.BlockSpec(memory_space=pltpu.HBM)],
        out_specs=(vmem,) * 4,
        scratch_shapes=[
            pltpu.VMEM((2, depth, SUB, width), jnp.float32),
            pltpu.SemaphoreType.DMA((4,)),
        ],
        name="edges",
    )(field)


def march_body(
    offsets, table, field_hbm, mats_hbm, z_first, z_second, y_first, y_second,
    first, own, spill, field, mats, weight, keep, spread, halves, sems,
):
    depth, rows, width = field_hbm.shape
    strips = width // LANES
    groups = rows // GROUP
    cols = [slice(j * LANES, (j + 1) * LANES) for j in range(strips)]

    def arrivals(kind, g):
        start = g * GROUP
        for j in range(strips):
            lanes = pl.ds(j * LANES, LANES)
            if kind == 0:
                yield pltpu.make_async_copy(
                    field_hbm.at[:, pl.ds(start, GROUP), lanes],
                    field.at[pl.ds(1, depth), j, pl.ds(SUB + start, GROUP), :],
                    sems.at[0, g, j],
                )
            else:
                yield pltpu.make_async_copy(
                    mats_hbm.at[:, pl.ds(start, GROUP), lanes],
                    mats.at[:, j, pl.ds(start, GROUP), :],
                    sems.at[1, g, j],
                )

    for g in range(groups):
        for kind in range(2):
            for copy in arrivals(kind, g):
                copy.start()
    z_even, y_even = is_even("depth"), is_even("area")
    first_plane = jnp.where(z_even, depth + 1, 0)
    second_plane = jnp.where(z_even, 0, depth + 1)
    for j in range(strips):
        field[first_plane, j, SUB : SUB + rows, :] = z_first[:, cols[j]]
        field[second_plane, j, SUB : SUB + rows, :] = z_second[:, cols[j]]
        one, two = y_first[:, cols[j]], y_second[:, cols[j]]
        field[1 : depth + 1, j, SUB - 1, :] = jnp.where(y_even, two, one)
        field[1 : depth + 1, j, SUB + rows, :] = jnp.where(y_even, one, two)
    spread[...] = jnp.zeros_like(spread)
    lane = lax.broadcasted_iota(jnp.int32, (SUB, LANES), 1)
    entry = lax.broadcasted_iota(jnp.int32, (SUB, LANES), 0)
    left_end = lane == 0
    right_end = lane == LANES - 1
    zero = jnp.zeros((SUB, LANES), jnp.float32)
    for c in range(4):
        for half in range(2):
            rows_of = zero
            for e in range(SUB):
                rows_of = jnp.where(entry == e, table[c, half * SUB + e], rows_of)
            halves[c, half] = rows_of if c == 3 else SHADE_UNIT * rows_of
    shift = offsets[lax.axis_index("depth")]

    def table_of(c):
        return halves[c, 0], halves[c, 1]

    def tile(i, unused):
        r = pl.multiple_of(i * SUB, SUB)

        def cells(z, unused):
            f = [field[z + 1, j, pl.ds(SUB + r, SUB), :] for j in range(strips)]
            from_left = [pltpu.roll(v, 1, 1) for v in f]
            from_right = [pltpu.roll(v, LANES - 1, 1) for v in f]
            for j in range(strips):
                above = field[z + 2, j, pl.ds(SUB + r, SUB), :]
                below = field[z, j, pl.ds(SUB + r, SUB), :]
                dz = above - below
                dy = (
                    field[z + 1, j, pl.ds(SUB + r + 1, SUB), :]
                    - field[z + 1, j, pl.ds(SUB + r - 1, SUB), :]
                )
                left = jnp.where(left_end, from_left[j - 1] if j else zero, from_left[j])
                right = jnp.where(
                    right_end, from_right[j + 1] if j < strips - 1 else zero, from_right[j]
                )
                dx = right - left
                grad_sq = 0.25 * (dz * dz + dy * dy + dx * dx)
                slope = jnp.abs(dz + (0.6 / 0.48) * dy + (0.64 / 0.48) * dx)
                shade = (0.3 / SHADE_UNIT) + slope * lax.rsqrt(grad_sq + 1.0)
                clear = jnp.exp2((-0.25 * LOG2E) * (f[j] * f[j] + grad_sq))
                most = lookup(table_of(3), mats[z, j, pl.ds(r, SUB), :])
                opacity = most - most * clear
                weight[z, j] = shade * opacity
                keep[z, j] = 1.0 - opacity
            return unused

        lax.fori_loop(0, depth, cells, 0, unroll=16)
        for j0 in range(0, strips, 2):
            colours = [table_of(c) for c in range(3)]

            def step(z, carry):
                result = []
                for k, (passed, front, back) in enumerate(carry):
                    j = j0 + k
                    w = weight[z, j]
                    kept = keep[z, j]
                    seen = w * passed
                    idx = mats[z, j, pl.ds(r, SUB), :]
                    looked = [lookup(t, idx) for t in colours]
                    result.append(
                        (
                            passed * kept,
                            [front[c] + looked[c] * seen for c in range(3)],
                            [back[c] * kept + looked[c] * w for c in range(3)],
                        )
                    )
                return result

            start = [(zero + 1.0, [zero] * 3, [zero] * 3)] * 2
            done = lax.fori_loop(0, depth, step, start, unroll=16)
            for k, (passed, front, back) in enumerate(done):
                j = j0 + k
                place = pl.ds(shift + r, SUB)
                for c in range(3):
                    put(first, i, c, cols[j], front[c])
                    spread[c, j, place, :] = back[c]
                put(first, i, 3, cols[j], 1.0 - passed)
                spread[3, j, place, :] = 1.0 - passed
        return unused

    for copy in arrivals(0, 0):
        copy.wait()

    def group(g, unused):
        for copy in arrivals(1, g):
            copy.wait()

        @pl.when(g + 1 < groups)
        def _():
            for copy in arrivals(0, g + 1):
                copy.wait()

        return lax.fori_loop(g * (GROUP // SUB), (g + 1) * (GROUP // SUB), tile, unused)

    lax.fori_loop(0, groups, group, 0)

    def hand_out(i, unused):
        r = pl.multiple_of(i * SUB, SUB)
        for c in range(4):
            for j in range(strips):
                put(own, i, c, cols[j], spread[c, j, pl.ds(r, SUB), :])
                put(spill, i, c, cols[j], spread[c, j, pl.ds(rows + r, SUB), :])
        return unused

    lax.fori_loop(0, rows // SUB, hand_out, 0)


def march(offsets, table, field, mats, rims, receivers):
    depth, rows, width = field.shape
    strips = width // LANES
    vmem = pl.BlockSpec(memory_space=pltpu.VMEM)
    smem = pl.BlockSpec(memory_space=pltpu.SMEM)
    hbm = pl.BlockSpec(memory_space=pltpu.HBM)
    image = jax.ShapeDtypeStruct((receivers, 4, rows // receivers, width), jnp.float32)
    return pl.pallas_call(
        march_body,
        out_shape=(image, image, image),
        in_specs=[smem, smem, hbm, hbm] + [vmem] * 4,
        out_specs=(vmem, vmem, vmem),
        scratch_shapes=[
            pltpu.VMEM((depth + 2, strips, rows + 2 * SUB, LANES), jnp.float32),
            pltpu.VMEM((depth, strips, rows, LANES), jnp.int32),
            pltpu.VMEM((depth, strips, SUB, LANES), jnp.float32),
            pltpu.VMEM((depth, strips, SUB, LANES), jnp.float32),
            pltpu.VMEM((4, strips, 2 * rows, LANES), jnp.float32),
            pltpu.VMEM((4, 2, SUB, LANES), jnp.float32),
            pltpu.SemaphoreType.DMA((2, rows // GROUP, strips)),
        ],
        cost_estimate=pl.CostEstimate(flops=10**8, bytes_accessed=10**7, transcendentals=10**6),
        name="march",
    )(offsets, table, field, mats, *rims)


def composite_body(order, stack, out):
    layers = stack.shape[0]
    for view in range(out.shape[0]):
        seen = jnp.ones(stack.shape[2:], jnp.float32)
        colour = [jnp.zeros(stack.shape[2:], jnp.float32)] * 3
        for k in range(layers):
            layer = order[view, k]
            colour = [colour[c] + seen * stack[layer, 4 * view + c] for c in range(3)]
            seen = seen - seen * stack[layer, 4 * view + 3]
        for c in range(3):
            out[view, c] = colour[c]
        out[view, 3] = 1.0 - seen


def composite(order, stack):
    vmem = pl.BlockSpec(memory_space=pltpu.VMEM)
    return pl.pallas_call(
        composite_body,
        out_shape=jax.ShapeDtypeStruct((2, 4) + stack.shape[2:], jnp.float32),
        in_specs=[pl.BlockSpec(memory_space=pltpu.SMEM), vmem],
        out_specs=vmem,
        name="composite",
    )(order, stack)


def swapped(block, axis, start):
    pairs = [(i, i + 1) for i in range(start, lax.axis_size(axis) - 1, 2)]
    return lax.ppermute(block, axis, pairs + [(b, a) for a, b in pairs])


def shards(field, materials, tf_table, view_order, shear_offset):
    receivers = lax.axis_size("depth")
    z_first, z_second, y_first, y_second = edges(field)
    rims = (
        swapped(z_first, "depth", 0),
        swapped(z_second, "depth", 1),
        swapped(y_first, "area", 0),
        swapped(y_second, "area", 1),
    )
    first, own, spill = march(shear_offset, tf_table, field, materials, rims, receivers)
    columns = lax.axis_size("area")
    arrived = lax.ppermute(spill, "area", [(i, i + 1) for i in range(columns - 1)])
    both = jnp.concatenate([first, own + arrived], axis=1)
    stack = lax.all_to_all(both, "depth", split_axis=0, concat_axis=0, tiled=True)
    return composite(view_order, stack)


def solution(mesh):
    in_specs = (P("depth", "area", None), P("depth", "area", None), P(), P(), P())
    out_specs = P(None, None, ("area", "depth"), None)
    return jax.shard_map(shards, mesh=mesh, in_specs=in_specs, out_specs=out_specs, check_vma=False)
```

```python
import jax
import jax.numpy as jnp
from jax import lax
from jax.experimental import pallas as pl
from jax.experimental.pallas import tpu as pltpu
from jax.sharding import PartitionSpec as P

LANES, SUB, GROUP = 128, 8, 8
HALO_ORDER = ("z_1", "y_1", "z_0", "y_0")
SMALL = pltpu.CompilerParams(vmem_limit_bytes=16 << 20)
LOG2E = 1.4426950408889634
SHADE_UNIT = 0.7 * 0.5 * 0.48

LOOKUP = lax.GatherDimensionNumbers(
    offset_dims=(),
    collapsed_slice_dims=(0,),
    start_index_map=(0,),
    operand_batching_dims=(1,),
    start_indices_batching_dims=(1,),
)


def lookup(halves, idx):
    place = (idx & (SUB - 1))[:, :, None]
    low, high = (
        lax.gather(half, place, LOOKUP, (1, 1), mode=lax.GatherScatterMode.PROMISE_IN_BOUNDS)
        for half in halves
    )
    return jnp.where(idx >= SUB, high, low)


def put(ref, tile, channel, cols, value):
    own = ref.shape[2]
    if own >= SUB:
        per = own // SUB
        if per == 1:
            ref[tile, channel, :, cols] = value
        else:
            ref[tile // per, channel, pl.ds(pl.multiple_of((tile % per) * SUB, SUB), SUB), cols] = value
    else:
        for part in range(SUB // own):
            ref[tile * (SUB // own) + part, channel, :, cols] = value[part * own : (part + 1) * own]


def is_even(axis):
    return lax.rem(lax.axis_index(axis), 2) == 0


def edges_body(field_hbm, z_first, z_second, y_first, y_second, rim, sems):
    depth, rows, _ = field_hbm.shape
    z_even, y_even = is_even("depth"), is_even("area")
    copies = [
        pltpu.make_async_copy(field_hbm.at[jnp.where(z_even, depth - 1, 0)], z_first, sems.at[0]),
        pltpu.make_async_copy(field_hbm.at[jnp.where(z_even, 0, depth - 1)], z_second, sems.at[1]),
        pltpu.make_async_copy(field_hbm.at[:, pl.ds(0, SUB), :], rim.at[0], sems.at[2]),
        pltpu.make_async_copy(field_hbm.at[:, pl.ds(rows - SUB, SUB), :], rim.at[1], sems.at[3]),
    ]
    for copy in copies:
        copy.start()
    for copy in copies[2:]:
        copy.wait()
    low, high = rim[0, :, 0, :], rim[1, :, SUB - 1, :]
    y_first[...] = jnp.where(y_even, high, low)
    y_second[...] = jnp.where(y_even, low, high)
    for copy in copies[:2]:
        copy.wait()


def edges(field):
    depth, rows, width = field.shape
    vmem = pl.BlockSpec(memory_space=pltpu.VMEM)
    plane = jax.ShapeDtypeStruct((rows, width), jnp.float32)
    wall = jax.ShapeDtypeStruct((depth, width), jnp.float32)
    return pl.pallas_call(
        edges_body,
        out_shape=(plane, plane, wall, wall),
        in_specs=[pl.BlockSpec(memory_space=pltpu.HBM)],
        out_specs=(vmem,) * 4,
        scratch_shapes=[
            pltpu.VMEM((2, depth, SUB, width), jnp.float32),
            pltpu.SemaphoreType.DMA((4,)),
        ],
        name="edges",
    )(field)


def march_body(
    offsets, table, field_hbm, mats_hbm, z_first, z_second, y_first, y_second,
    *refs,
):
    *parts, field, mats, weight, keep, image, wrapped, spread, halves, sems = refs
    depth, rows, width = field_hbm.shape
    strips = width // LANES
    groups = rows // GROUP
    cols = [slice(j * LANES, (j + 1) * LANES) for j in range(strips)]

    def arrivals(kind, g):
        start = g * GROUP
        for j in range(strips):
            lanes = pl.ds(j * LANES, LANES)
            if kind == 0:
                yield pltpu.make_async_copy(
                    field_hbm.at[:, pl.ds(start, GROUP), lanes],
                    field.at[pl.ds(1, depth), j, pl.ds(SUB + start, GROUP), :],
                    sems.at[0, g, j],
                )
            else:
                yield pltpu.make_async_copy(
                    mats_hbm.at[:, pl.ds(start, GROUP), lanes],
                    mats.at[:, j, pl.ds(start, GROUP), :],
                    sems.at[1, g, j],
                )

    for g in range(groups):
        for kind in range(2):
            for copy in arrivals(kind, g):
                copy.start()
    z_even, y_even = is_even("depth"), is_even("area")
    first_plane = jnp.where(z_even, depth + 1, 0)
    second_plane = jnp.where(z_even, 0, depth + 1)
    for j in range(strips):
        field[first_plane, j, SUB : SUB + rows, :] = z_first[:, cols[j]]
        field[second_plane, j, SUB : SUB + rows, :] = z_second[:, cols[j]]
        one, two = y_first[:, cols[j]], y_second[:, cols[j]]
        field[1 : depth + 1, j, SUB - 1, :] = jnp.where(y_even, two, one)
        field[1 : depth + 1, j, SUB + rows, :] = jnp.where(y_even, one, two)
    spread[...] = jnp.zeros_like(spread)
    lane = lax.broadcasted_iota(jnp.int32, (SUB, LANES), 1)
    entry = lax.broadcasted_iota(jnp.int32, (SUB, LANES), 0)
    left_end = lane == 0
    right_end = lane == LANES - 1
    zero = jnp.zeros((SUB, LANES), jnp.float32)
    for c in range(4):
        for half in range(2):
            rows_of = zero
            for e in range(SUB):
                rows_of = jnp.where(entry == e, table[c, half * SUB + e], rows_of)
            halves[c, half] = rows_of if c == 3 else SHADE_UNIT * rows_of
    shift = offsets[lax.axis_index("depth")]

    def table_of(c):
        return halves[c, 0], halves[c, 1]

    def tile(i, unused):
        r = pl.multiple_of(i * SUB, SUB)

        def cells(z, unused):
            f = [field[z + 1, j, pl.ds(SUB + r, SUB), :] for j in range(strips)]
            from_left = [pltpu.roll(v, 1, 1) for v in f]
            from_right = [pltpu.roll(v, LANES - 1, 1) for v in f]
            for j in range(strips):
                above = field[z + 2, j, pl.ds(SUB + r, SUB), :]
                below = field[z, j, pl.ds(SUB + r, SUB), :]
                dz = above - below
                dy = (
                    field[z + 1, j, pl.ds(SUB + r + 1, SUB), :]
                    - field[z + 1, j, pl.ds(SUB + r - 1, SUB), :]
                )
                left = jnp.where(left_end, from_left[j - 1] if j else zero, from_left[j])
                right = jnp.where(
                    right_end, from_right[j + 1] if j < strips - 1 else zero, from_right[j]
                )
                dx = right - left
                grad_sq = 0.25 * (dz * dz + dy * dy + dx * dx)
                slope = jnp.abs(dz + (0.6 / 0.48) * dy + (0.64 / 0.48) * dx)
                shade = (0.3 / SHADE_UNIT) + slope * lax.rsqrt(grad_sq + 1.0)
                clear = jnp.exp2((-0.25 * LOG2E) * (f[j] * f[j] + grad_sq))
                most = lookup(table_of(3), mats[z, j, pl.ds(r, SUB), :])
                opacity = most - most * clear
                weight[z, j] = shade * opacity
                keep[z, j] = 1.0 - opacity
            return unused

        lax.fori_loop(0, depth, cells, 0, unroll=16)
        for j0 in range(0, strips, 2):
            colours = [table_of(c) for c in range(3)]

            def step(z, carry):
                result = []
                for k, (passed, front, back) in enumerate(carry):
                    j = j0 + k
                    w = weight[z, j]
                    kept = keep[z, j]
                    seen = w * passed
                    idx = mats[z, j, pl.ds(r, SUB), :]
                    looked = [lookup(t, idx) for t in colours]
                    result.append(
                        (
                            passed * kept,
                            [front[c] + looked[c] * seen for c in range(3)],
                            [back[c] * kept + looked[c] * w for c in range(3)],
                        )
                    )
                return result

            start = [(zero + 1.0, [zero] * 3, [zero] * 3)] * 2
            done = lax.fori_loop(0, depth, step, start, unroll=16)
            for k, (passed, front, back) in enumerate(done):
                j = j0 + k
                place = pl.ds(shift + r, SUB)
                for c in range(3):
                    put(image, i, c, cols[j], front[c])
                    spread[c, j, place, :] = back[c]
                put(image, i, 3, cols[j], 1.0 - passed)
                spread[3, j, place, :] = 1.0 - passed
        return unused

    for copy in arrivals(0, 0):
        copy.wait()

    def group(g, unused):
        for copy in arrivals(1, g):
            copy.wait()

        @pl.when(g + 1 < groups)
        def _():
            for copy in arrivals(0, g + 1):
                copy.wait()

        return lax.fori_loop(g * (GROUP // SUB), (g + 1) * (GROUP // SUB), tile, unused)

    lax.fori_loop(0, groups, group, 0)

    def hand_out(i, unused):
        r = pl.multiple_of(i * SUB, SUB)
        for c in range(4):
            for j in range(strips):
                both = spread[c, j, pl.ds(r, SUB), :] + spread[c, j, pl.ds(rows + r, SUB), :]
                put(wrapped, i, c, cols[j], both)
        return unused

    lax.fori_loop(0, rows // SUB, hand_out, 0)
    me = lax.axis_index("depth")
    for part, (step, views) in zip(parts, shipments(image.shape[0])):
        for k, view in enumerate(views):
            part[4 * k : 4 * k + 4] = (image, wrapped)[view][me ^ step]


def shipments(receivers):
    far = range(receivers - 1, receivers // 2 - 1, -1)
    near = range(receivers // 2 - 1, -1, -1)
    return [(s, (1,)) for s in far] + [(s, (0, 1)) for s in near if s] + [
        (s, (0,)) for s in far
    ] + [(0, (0, 1))]


def march(offsets, table, field, mats, rims, receivers):
    depth, rows, width = field.shape
    strips = width // LANES
    vmem = pl.BlockSpec(memory_space=pltpu.VMEM)
    smem = pl.BlockSpec(memory_space=pltpu.SMEM)
    hbm = pl.BlockSpec(memory_space=pltpu.HBM)
    tall = rows // receivers
    plan = shipments(receivers)
    image = pltpu.VMEM((receivers, 4, tall, width), jnp.float32)
    return pl.pallas_call(
        march_body,
        out_shape=[
            jax.ShapeDtypeStruct((4 * len(views), tall, width), jnp.float32) for _, views in plan
        ],
        in_specs=[smem, smem, hbm, hbm] + [vmem] * 4,
        out_specs=[vmem] * len(plan),
        scratch_shapes=[
            pltpu.VMEM((depth + 2, strips, rows + 2 * SUB, LANES), jnp.float32),
            pltpu.VMEM((depth, strips, rows, LANES), jnp.int32),
            pltpu.VMEM((depth, strips, SUB, LANES), jnp.float32),
            pltpu.VMEM((depth, strips, SUB, LANES), jnp.float32),
            image,
            image,
            pltpu.VMEM((4, strips, 2 * rows, LANES), jnp.float32),
            pltpu.VMEM((4, 2, SUB, LANES), jnp.float32),
            pltpu.SemaphoreType.DMA((2, rows // GROUP, strips)),
        ],
        compiler_params=pltpu.CompilerParams(vmem_limit_bytes=40 << 20),
        cost_estimate=pl.CostEstimate(flops=10**8, bytes_accessed=10**7, transcendentals=10**6),
        name="march",
    )(offsets, table, field, mats, *rims)


def collect_body(*refs):
    *parts, own, stack = refs
    stack[0] = own[4:8]
    for step, part in enumerate(parts, 1):
        stack[step] = part[part.shape[0] - 4 :]


def collect(parts, own):
    vmem = pl.BlockSpec(memory_space=pltpu.VMEM)
    shape = (len(parts) + 1, 4) + own.shape[1:]
    return pl.pallas_call(
        collect_body,
        out_shape=jax.ShapeDtypeStruct(shape, jnp.float32),
        in_specs=[vmem] * (len(parts) + 1),
        out_specs=vmem,
        compiler_params=SMALL,
        name="collect",
    )(*parts, own)


def over(order, view, footprint, out):
    shape = out.shape[2:]
    seen = jnp.ones(shape, jnp.float32)
    colour = [jnp.zeros(shape, jnp.float32)] * 3
    for k in range(order.shape[1]):
        *colours, opacity = footprint(order[view, k])
        colour = [old + seen * new for old, new in zip(colour, colours)]
        seen = seen - seen * opacity
    for c in range(3):
        out[view, c] = colour[c]
    out[view, 3] = 1.0 - seen


def sheared_body(order, offsets, own_hbm, odd_hbm, even_hbm, out, own, arrived, sems):
    own_copy = pltpu.make_async_copy(own_hbm, own, sems.at[0])
    own_copy.start()
    even = is_even("area")

    @pl.when(even)
    def _():
        pltpu.make_async_copy(even_hbm, arrived, sems.at[1]).start()

    @pl.when(jnp.logical_not(even))
    def _():
        pltpu.make_async_copy(odd_hbm, arrived, sems.at[1]).start()

    own_copy.wait()
    pltpu.make_async_copy(even_hbm, arrived, sems.at[1]).wait()
    tall = own.shape[2]
    row = lax.axis_index("depth") * tall + lax.broadcasted_iota(jnp.int32, own.shape[2:], 0)

    def footprint(layer):
        moved = row >= offsets[layer]
        place = layer ^ lax.axis_index("depth")
        return [jnp.where(moved, own[place, c], arrived[place, c]) for c in range(4)]

    over(order, 1, footprint, out)


def sheared(order, offsets, own, odd, even):
    vmem = pl.BlockSpec(memory_space=pltpu.VMEM)
    smem = pl.BlockSpec(memory_space=pltpu.SMEM)
    hbm = pl.BlockSpec(memory_space=pltpu.HBM)
    return pl.pallas_call(
        sheared_body,
        out_shape=jax.ShapeDtypeStruct((2,) + own.shape[1:], jnp.float32),
        in_specs=[smem, smem, hbm, hbm, hbm],
        out_specs=vmem,
        scratch_shapes=[pltpu.VMEM(own.shape, jnp.float32)] * 2 + [pltpu.SemaphoreType.DMA((2,))],
        compiler_params=SMALL,
        name="sheared",
    )(order, offsets, own, odd, even)


def straight_body(order, done, *refs):
    *parts, out, stack = refs
    for step, part in enumerate(parts):
        stack[step] = part[0:4]
    me = lax.axis_index("depth")
    over(order, 0, lambda layer: [stack[layer ^ me, c] for c in range(4)], out)
    out[1] = done[1]


def straight(order, done, parts):
    vmem = pl.BlockSpec(memory_space=pltpu.VMEM)
    return pl.pallas_call(
        straight_body,
        out_shape=jax.ShapeDtypeStruct(done.shape, jnp.float32),
        in_specs=[pl.BlockSpec(memory_space=pltpu.SMEM)] + [vmem] * (len(parts) + 1),
        out_specs=vmem,
        scratch_shapes=[pltpu.VMEM((len(parts), 4) + parts[0].shape[1:], jnp.float32)],
        compiler_params=SMALL,
        name="straight",
    )(order, done, *parts)


def swapped(block, axis, start):
    pairs = [(i, i + 1) for i in range(start, lax.axis_size(axis) - 1, 2)]
    return lax.ppermute(block, axis, pairs + [(b, a) for a, b in pairs])


def shards(field, materials, tf_table, view_order, shear_offset):
    receivers = lax.axis_size("depth")
    field = pltpu.with_memory_space_constraint(field, pltpu.HBM)
    materials = pltpu.with_memory_space_constraint(materials, pltpu.HBM)
    blocks = dict(zip(("z_0", "z_1", "y_0", "y_1"), edges(field)))
    for name in HALO_ORDER:
        axis = "depth" if name[0] == "z" else "area"
        blocks[name] = swapped(blocks[name], axis, int(name[2]))
    *parts, own = march(
        shear_offset, tf_table, field, materials, blocks.values(), receivers
    )
    straight_parts, turned_parts = {0: own}, {}
    for part, (step, views) in zip(parts, shipments(receivers)):
        route = [(i, i ^ step) for i in range(receivers)]
        part = lax.ppermute(part, "depth", route)
        if 0 in views:
            straight_parts[step] = part
        if 1 in views:
            turned_parts[step] = part
    stack = collect([turned_parts[s] for s in range(1, receivers)], own)
    columns = lax.axis_size("area")
    odd = lax.ppermute(stack, "area", [(i, i + 1) for i in range(0, columns - 1, 2)])
    even = lax.ppermute(stack, "area", [(i, i + 1) for i in range(1, columns - 1, 2)])
    done = sheared(view_order, shear_offset, stack, odd, even)
    return straight(view_order, done, [straight_parts[s] for s in range(receivers)])


def solution(mesh):
    in_specs = (P("depth", "area", None), P("depth", "area", None), P(), P(), P())
    out_specs = P(None, None, ("area", "depth"), None)
    return jax.shard_map(shards, mesh=mesh, in_specs=in_specs, out_specs=out_specs, check_vma=False)
```
